512 devices in a mesh: ctx: 32 (over z, y_lo), tp: 16 (over y_hi, x, core).
Axes of the slice: x: 4, y: 4 (y_hi: 2, y_lo: 2; y = y_hi * 2 + y_lo), z: 16, core: 2. Of those that a mesh axis runs over, the one named last changes fastest.
Arguments:
- gate_in: bfloat16 [4096, 4096], P('ctx', 'tp'), may hold values from -250 to 250, as said below
- conv_in: bfloat16 [4096, 4096], P('ctx', 'tp'), may hold values from -6 to 6
- value_in: bfloat16 [4096, 4096], P('ctx', 'tp'), may hold values from -6 to 6
- filter_taps: float32 [128, 4096], P(None, 'tp'), may hold values from -0.5 to 0.5
- norm_gain: float32 [4096], P('tp'), may hold values from 0.1 to 1.9
- qkv_weight: bfloat16 [4096, 3, 2048], P(None, None, 'tp'), may hold values from -0.5 to 0.5
Outputs:
- attended: bfloat16 [4096, 2048], P('ctx', 'tp')
The draws below stay inside these ranges and needn't reach their ends.
Inputs may be any that keep to these rules, and one draw needn't show every extreme that they name: `gate_in`: gate values; channels and bases carry different scales.
All inputs are finite; a program needn't handle non-finite values.
Results may differ from the reference program's by a relative error of at most 0.027.
Values may be sent and summed in bfloat16 or wider, within the bound.
A program may use at most 128 MiB of HBM per device.

```python
import math
import jax
import jax.numpy as jnp
from jax import lax

D = 4096
FILTER = 128
HEAD_DIM = 128
HEADS = 16
LENGTH = 4096


def draw_gate_in(key, part):
    first, second = jax.random.split(key, 2)
    base = jnp.clip(jax.random.normal(first, (LENGTH, D), jnp.float32), -6.0, 6.0)
    channel_scale = jnp.exp(jnp.log(10.0) * jnp.arange(D, dtype=jnp.float32) / D)
    row_scale = jnp.exp(jnp.log(10.0) * jax.random.uniform(second, (LENGTH, 1), jnp.float32))
    return (base * channel_scale[None, :] * row_scale / 2.5).astype(jnp.bfloat16)


def draw_qkv_weight(key, part):
    first = jax.random.fold_in(key, 0)
    width = HEADS * HEAD_DIM
    base = jnp.clip(jax.random.normal(first, (D, 3, width), jnp.float32), -6.0, 6.0) * D ** (-0.5)
    base = jnp.clip(base, -0.5, 0.5)
    return base.astype(jnp.bfloat16)


def shard_levels(own_key, extent, shards, least, high):
    level = 1.0
    for position, parts in shards:
        heights = jax.random.uniform(jax.random.fold_in(jax.random.fold_in(own_key, 6), position), (parts,), jnp.float32, least / len(shards), high / len(shards))
        level = level * jnp.repeat(jnp.exp(heights), extent[position] // parts).reshape((-1,) + (1,) * (len(extent) - 1 - position))
    return level


def normal_values(key, dims, spread, bound, pieces=(), kind=jnp.bfloat16):
    values = jax.random.normal(key, dims, jnp.float32) * spread
    if len(pieces) > 0:
        values = shard_levels(key, dims, pieces, -0.22, 0.18) * values
    return jnp.clip(values, min=-bound, max=bound).astype(kind)


def setup_inputs(seed: int = 0) -> dict:
    arg_keys = jax.random.split(jax.random.key(seed), 7)
    return {
        "gate_in": draw_gate_in(jax.random.fold_in(arg_keys[6], 71), 0),
        "conv_in": normal_values(arg_keys[1], (LENGTH, D), 1.0, 6.0, ((0, 32), (1, 16))),
        "value_in": normal_values(arg_keys[2], (LENGTH, D), 1.0, 6.0, ((0, 32), (1, 16))),
        "filter_taps": normal_values(arg_keys[3], (FILTER, D), FILTER ** -0.5, 0.5, ((1, 16),), jnp.float32),
        "norm_gain": jnp.clip(1.0 + 0.18 * jax.random.normal(arg_keys[4], (D,), jnp.float32), 0.1, 1.9),
        "qkv_weight": draw_qkv_weight(jax.random.fold_in(arg_keys[6], 71), 0),
    }


def causal_filter(full, taps):
    span = taps.shape[0]
    channels = full.shape[1]
    group = math.gcd(channels, 64)
    nblocks = full.shape[0] // span
    blocks = full.reshape(nblocks, span, channels)
    diff = jnp.arange(span, dtype=jnp.int32)[:, None] - jnp.arange(span, dtype=jnp.int32)[None, :]
    cur_idx = jnp.clip(diff, 0, span - 1)
    prev_idx = jnp.clip(diff + span, 0, span - 1)

    def one_group(start):
        tgroup = lax.dynamic_slice_in_dim(taps, start, group, 1)
        tcur = jnp.where((diff >= 0)[:, :, None], tgroup[cur_idx], 0.0)
        tprev = jnp.where((diff < 0)[:, :, None], tgroup[prev_idx], 0.0)
        bgroup = lax.dynamic_slice_in_dim(blocks, start, group, 2)
        out = jnp.einsum('bsc,isc->bic', bgroup[1:], tcur, precision=lax.Precision.HIGHEST)
        out = out + jnp.einsum('bsc,isc->bic', bgroup[:-1], tprev, precision=lax.Precision.HIGHEST)
        return out
    starts = (jnp.arange(channels // group) * group).astype(jnp.int32)
    result = lax.map(one_group, starts)
    return result.transpose(1, 2, 0, 3).reshape((nblocks - 1) * span, channels)

def reference(gate_in, conv_in, value_in, filter_taps, norm_gain, qkv_weight):
    mixed = (conv_in.astype(jnp.float32) * value_in.astype(jnp.float32)).astype(jnp.bfloat16)
    mixed = lax.optimization_barrier(mixed).astype(jnp.float32)
    full = jnp.concatenate([jnp.zeros((FILTER, D), jnp.float32), mixed], axis=0)
    filtered = causal_filter(full, filter_taps)
    hyena = (gate_in.astype(jnp.float32) * filtered).astype(jnp.bfloat16)
    hyena = lax.optimization_barrier(hyena).astype(jnp.float32)
    msq = lax.optimization_barrier(jnp.mean(hyena * hyena, axis=1))
    normed = (hyena * lax.rsqrt(msq + 1e-06)[:, None] * norm_gain[None, :]).astype(jnp.bfloat16)
    flat = qkv_weight.reshape(D, 3 * HEADS * HEAD_DIM)
    proj = jnp.dot(normed, flat, preferred_element_type=jnp.float32).astype(jnp.bfloat16)
    proj = proj.reshape(LENGTH, 3, HEADS, HEAD_DIM)
    query = proj[:, 0].astype(jnp.float32)
    key = proj[:, 1].astype(jnp.float32)
    value = proj[:, 2].astype(jnp.float32)
    block = math.gcd(LENGTH, 128)
    key_pos = jnp.arange(LENGTH, dtype=jnp.int32)
    scale = 1.0 / math.sqrt(HEAD_DIM)

    def attend(start):
        qblock = lax.dynamic_slice_in_dim(query, start, block, 0)
        qpos = start + jnp.arange(block, dtype=jnp.int32)
        scores = jnp.einsum('qhd,khd->hqk', qblock, key) * scale
        allowed = (qpos[:, None] >= key_pos[None, :])[None]
        scores = jnp.where(allowed, scores, -1e+30)
        rowmax = lax.optimization_barrier(jnp.max(scores, axis=2, keepdims=True))
        expo = jnp.where(allowed, jnp.exp(scores - rowmax), 0.0)
        total = lax.optimization_barrier(jnp.sum(expo, axis=2))
        weights = expo.astype(jnp.bfloat16).astype(jnp.float32)
        out = jnp.einsum('hqk,khd->qhd', weights, value) / total.T[:, :, None]
        return out.astype(jnp.bfloat16)
    starts = (jnp.arange(LENGTH // block) * block).astype(jnp.int32)
    blocks = lax.map(attend, starts)
    return blocks.reshape(LENGTH, HEADS * HEAD_DIM)
```

```python
import math

import jax
import jax.numpy as jnp
from jax import lax
from jax.experimental import pallas as pl
from jax.experimental.pallas import tpu as pltpu
from jax.sharding import PartitionSpec as P

D = 4096
HEAD_DIM = 128
ROWS = 128
CH = 256
CTX = 32
TP = 16
NZ = 16
NEAR = 3
F32 = jnp.float32
BF16 = jnp.bfloat16


def flipped(index, bits):
    out = index
    for bit in (1, 2, 4, 8):
        if bits & bit:
            out = out + bit - 2 * bit * ((index // bit) % 2)
    return out


def kernel(
    gate_ref, conv_ref, value_ref, taps_ref, gain_ref, w_hbm, out_ref,
    mixed, rim, shifted, xall, gains, w_ref, kv, q_ref, proj, squares,
    top, total, acc,
    w_sem, rim_send, rim_recv, gain_send, gain_recv,
    x_send, x_recv, half_send, half_recv, kv_send, kv_recv,
):
    c = lax.axis_index("ctx")
    tp = lax.axis_index("tp")
    z = c // 2
    partner = c + 1 - 2 * (c % 2)
    after = (c + 1) % CTX
    before = (c + CTX - 1) % CTX
    up = (c + 2) % CTX
    down = (c + CTX - 2) % CTX

    w_copy = pltpu.make_async_copy(w_hbm, w_ref, w_sem)
    w_copy.start()

    barrier = pltpu.get_barrier_semaphore()
    for bits in range(1, TP):
        pl.semaphore_signal(barrier, inc=1, device_id={"tp": flipped(tp, bits)})
    for other in (after, before, partner, up, down):
        pl.semaphore_signal(barrier, inc=1, device_id={"ctx": other})
    mixed[...] = (conv_ref[...].astype(F32) * value_ref[...].astype(F32)).astype(BF16)
    pl.semaphore_wait(barrier, TP - 1 + 5)

    sent = []

    def send(src, dst, send_sem, recv_sem, where):
        copy = pltpu.make_async_remote_copy(
            src_ref=src, dst_ref=dst, send_sem=send_sem, recv_sem=recv_sem, device_id=where
        )
        copy.start()
        sent.append(copy)

    def arrived(dst, send_sem, recv_sem, where):
        pltpu.make_async_remote_copy(
            src_ref=dst, dst_ref=dst, send_sem=send_sem, recv_sem=recv_sem, device_id=where
        ).wait_recv()

    send(mixed, rim, rim_send, rim_recv, {"ctx": after})
    for bits in range(1, TP):
        send(
            gain_ref, gains.at[bits], gain_send.at[bits], gain_recv.at[bits],
            {"tp": flipped(tp, bits)},
        )
    gains[0] = gain_ref[...]

    arrived(rim, rim_send, rim_recv, {"ctx": before})
    first = (c > 0).astype(F32)
    full = jnp.concatenate([rim[...].astype(F32) * first, mixed[...].astype(F32)], axis=0)
    for r in range(8):
        shifted[r] = full if r == 0 else pltpu.roll(full, r, 0)

    def tap_group(q, carry):
        base = pl.multiple_of(ROWS - 8 * q, 8)
        rows = taps_ref[pl.ds(pl.multiple_of(8 * q, 8), 8), :]
        for r in range(8):
            carry = carry + rows[r : r + 1, :] * shifted[r, pl.ds(base, ROWS), :]
        return carry

    filtered = lax.fori_loop(0, 16, tap_group, jnp.zeros((ROWS, CH), F32))
    xall[0] = (gate_ref[...].astype(F32) * filtered).astype(BF16)

    def push(slot, bits):
        send(
            xall.at[slot], xall.at[slot ^ bits], x_send.at[len(sent)], x_recv.at[slot ^ bits],
            {"tp": flipped(tp, bits)},
        )

    def push_half(slot, half, bits):
        rows = pl.ds(64 * half, 64)
        send(
            xall.at[slot, rows], xall.at[slot ^ bits, rows],
            half_send.at[slot // 8, half], half_recv.at[slot // 8, half],
            {"tp": flipped(tp, bits)},
        )

    def await_slot(slot):
        if slot % 8 == 4:
            for half in range(2):
                rows = xall.at[slot, pl.ds(64 * half, 64)]
                arrived(
                    rows, half_send.at[slot // 8, half], half_recv.at[slot // 8, half],
                    {"tp": flipped(tp, 2)},
                )
        else:
            arrived(xall.at[slot], x_send.at[0], x_recv.at[slot], {"tp": flipped(tp, 1)})

    def absorb(slot):
        h = xall[slot].astype(F32)
        squared = h * h
        part = squared[:, :128] + squared[:, 128:]
        squares[...] = part if slot == 0 else squares[...] + part
        x = (h * gains[slot]).astype(BF16)
        start = pl.multiple_of(flipped(tp, slot) * CH, CH)
        for i in range(3):
            added = jnp.dot(x, w_ref[i, pl.ds(start, CH), :], preferred_element_type=F32)
            proj[i] = added if slot == 0 else proj[i] + added

    for bits in (8, 2, 6, 1):
        push(0, bits)
    w_copy.wait()
    absorb(0)
    for bits in range(1, TP):
        arrived(gains.at[bits], gain_send.at[bits], gain_recv.at[bits], {"tp": flipped(tp, bits)})
    await_slot(1)
    absorb(1)
    await_slot(2)
    push_half(2, 0, 6)
    push(2, 1)
    await_slot(6)
    push_half(6, 1, 2)
    push(6, 1)
    absorb(2)
    absorb(6)
    await_slot(8)
    push(8, 2)
    push(8, 6)
    push(8, 1)
    await_slot(4)
    push(4, 1)
    absorb(8)
    absorb(4)
    await_slot(3)
    absorb(3)
    await_slot(7)
    absorb(7)
    await_slot(10)
    push_half(10, 0, 6)
    push(10, 1)
    await_slot(14)
    push_half(14, 1, 2)
    push(14, 1)
    absorb(10)
    absorb(14)
    await_slot(9)
    absorb(9)
    await_slot(5)
    absorb(5)
    await_slot(12)
    push(12, 1)
    absorb(12)
    for slot in (11, 15, 13):
        await_slot(slot)
        absorb(slot)

    msq = jnp.sum(squares[...], axis=1, keepdims=True) / D
    factor = lax.rsqrt(msq + 1e-06)
    kv[c] = jnp.concatenate([proj[1] * factor, proj[2] * factor], axis=1).astype(BF16)
    q_ref[...] = (proj[0] * factor).astype(BF16)

    counter = [0]

    def pass_on(source, direction, lane, step, other):
        send(
            kv.at[source], kv.at[source], kv_send.at[counter[0]],
            kv_recv.at[direction, lane, step], {"ctx": other},
        )
        counter[0] += 1

    def await_block(source, direction, lane, step):
        arrived(kv.at[source], kv_send.at[0], kv_recv.at[direction, lane, step], {"ctx": partner})

    def source_of(first_index, direction, step):
        move = CTX - 2 * step if direction == 0 else 2 * step
        return (first_index + move) % CTX

    row_pos = c * ROWS + lax.broadcasted_iota(jnp.int32, (ROWS, 256), 0)
    key_iota = lax.broadcasted_iota(jnp.int32, (ROWS, 256), 1)
    scale = 1.0 / math.sqrt(HEAD_DIM)

    def attend(z_source, initial=False):
        pair = kv[pl.ds(2 * z_source, 2)].reshape(256, 256)
        scores = (
            lax.dot_general(
                q_ref[...], pair[:, :128], (((1,), (1,)), ((), ())), preferred_element_type=F32
            )
            * scale
        )
        allowed = row_pos >= key_iota + z_source * 256
        scores = jnp.where(allowed, scores, -1e30)
        block_top = jnp.max(scores, axis=1, keepdims=True)
        new_top = block_top if initial else jnp.maximum(top[...], block_top)
        expo = jnp.where(allowed, jnp.exp(scores - new_top), 0.0)
        block_total = jnp.sum(expo, axis=1, keepdims=True)
        added = jnp.dot(expo.astype(BF16), pair[:, 128:], preferred_element_type=F32)
        if initial:
            total[...] = block_total
            acc[...] = added
        else:
            fade = jnp.exp(top[...] - new_top)
            total[...] = total[...] * fade + block_total
            acc[...] = acc[...] * fade + added
        top[...] = new_top

    def attend_step(step):
        @pl.when(z >= step)
        def _():
            attend((z + NZ - step) % NZ)

        if step < 8:
            @pl.when(z + step >= NZ)
            def _():
                attend((z + step) % NZ)

    toward = (up, down)
    last_a = (8, 7)
    pass_on(c, 0, 0, 1, up)
    pass_on(c, 1, 0, 1, down)
    pass_on(c, 0, 1, 0, partner)
    await_block(partner, 0, 1, 0)
    pass_on(partner, 0, 1, 1, up)
    pass_on(partner, 1, 1, 1, down)
    attend(z, initial=True)
    for step in range(1, 10):
        for direction in range(2):
            if step <= last_a[direction]:
                source = source_of(c, direction, step)
                await_block(source, direction, 0, step)
                if step < last_a[direction]:
                    pass_on(source, direction, 0, step + 1, toward[direction])
                if step > NEAR:
                    pass_on(source, direction, 1, step, partner)
        ready = step if step <= NEAR else step - 1
        if step == NEAR + 1:
            continue
        for direction in range(2):
            if ready <= last_a[direction]:
                source = source_of(partner, direction, ready)
                await_block(source, direction, 1, ready)
                if ready < NEAR:
                    pass_on(source, direction, 1, ready + 1, toward[direction])
        attend_step(ready)

    out_ref[...] = (acc[...] / total[...]).astype(BF16)
    for copy in sent:
        copy.wait_send()


def body(gate_in, conv_in, value_in, filter_taps, norm_gain, qkv_weight):
    vmem = pl.BlockSpec(memory_space=pltpu.VMEM)
    dma = pltpu.SemaphoreType.DMA
    return pl.pallas_call(
        kernel,
        out_shape=jax.ShapeDtypeStruct((ROWS, HEAD_DIM), BF16),
        in_specs=[vmem] * 5 + [pl.BlockSpec(memory_space=pl.ANY)],
        out_specs=vmem,
        scratch_shapes=[
            pltpu.VMEM((ROWS, CH), BF16),
            pltpu.VMEM((ROWS, CH), BF16),
            pltpu.VMEM((8, 2 * ROWS, CH), F32),
            pltpu.VMEM((TP, ROWS, CH), BF16),
            pltpu.VMEM((TP, 1, CH), F32),
            pltpu.VMEM((3, D, HEAD_DIM), BF16),
            pltpu.VMEM((CTX, ROWS, 2 * HEAD_DIM), BF16),
            pltpu.VMEM((ROWS, HEAD_DIM), BF16),
            pltpu.VMEM((3, ROWS, HEAD_DIM), F32),
            pltpu.VMEM((ROWS, HEAD_DIM), F32),
            pltpu.VMEM((ROWS, 1), F32),
            pltpu.VMEM((ROWS, 1), F32),
            pltpu.VMEM((ROWS, HEAD_DIM), F32),
            dma,
            dma,
            dma,
            dma((TP,)),
            dma((TP,)),
            dma((48,)),
            dma((TP,)),
            dma((2, 2)),
            dma((2, 2)),
            dma((48,)),
            dma((2, 2, 9)),
        ],
        compiler_params=pltpu.CompilerParams(collective_id=0, has_side_effects=True),
    )(
        gate_in, conv_in, value_in, filter_taps, norm_gain.reshape(1, CH),
        jnp.transpose(qkv_weight, (1, 0, 2)),
    )


def solution(mesh):
    placed = (
        P("ctx", "tp"),
        P("ctx", "tp"),
        P("ctx", "tp"),
        P(None, "tp"),
        P("tp"),
        P(None, None, "tp"),
    )
    return jax.shard_map(
        body, mesh=mesh, in_specs=placed, out_specs=P("ctx", "tp"), check_vma=False
    )
```

```python
import math

import jax
import jax.numpy as jnp
from jax import lax
from jax.experimental import pallas as pl
from jax.experimental.pallas import tpu as pltpu
from jax.sharding import PartitionSpec as P

D = 4096
HEAD_DIM = 128
ROWS = 128
CH = 256
CTX = 32
TP = 16
NZ = 16
NEAR = 1
PIECES = 2
PARENT = {far: far - 1 for far in range(1, 9)}
HOPS = sorted({far - near for far, near in PARENT.items()})
F32 = jnp.float32
BF16 = jnp.bfloat16


def flipped(index, bits):
    out = index
    for bit in (1, 2, 4, 8):
        if bits & bit:
            out = out + bit - 2 * bit * ((index // bit) % 2)
    return out


def kernel(
    gate_ref, conv_ref, value_ref, taps_ref, gain_ref, w_hbm, out_ref,
    mixed, rim, shifted, filtered, xall, gains, w_ref, kv, q_ref, proj, squares,
    top, total, acc,
    w_sem, rim_send, rim_recv, gain_send, gain_recv,
    x_send, x_recv, half_send, half_recv, kv_send, kv_recv,
):
    c = lax.axis_index("ctx")
    tp = lax.axis_index("tp")
    z = c // 2
    partner = c + 1 - 2 * (c % 2)
    after = (c + 1) % CTX
    before = (c + CTX - 1) % CTX

    def along(direction, hops):
        return (c + (2 * hops if direction == 0 else CTX - 2 * hops)) % CTX


    w_copy = pltpu.make_async_copy(w_hbm, w_ref, w_sem)
    w_copy.start()

    barrier = pltpu.get_barrier_semaphore()
    for bits in range(1, TP):
        pl.semaphore_signal(barrier, inc=1, device_id={"tp": flipped(tp, bits)})
    ringed = [along(direction, hops) for hops in HOPS for direction in range(2)]
    for other in [after, before, partner] + ringed:
        pl.semaphore_signal(barrier, inc=1, device_id={"ctx": other})
    mixed[...] = (conv_ref[...].astype(F32) * value_ref[...].astype(F32)).astype(BF16)
    pl.semaphore_wait(barrier, TP - 1 + 3 + 2 * len(HOPS))

    sent = []

    def send(src, dst, send_sem, recv_sem, where):
        copy = pltpu.make_async_remote_copy(
            src_ref=src, dst_ref=dst, send_sem=send_sem, recv_sem=recv_sem, device_id=where
        )
        copy.start()
        sent.append(copy)

    def arrived(dst, send_sem, recv_sem, where):
        pltpu.make_async_remote_copy(
            src_ref=dst, dst_ref=dst, send_sem=send_sem, recv_sem=recv_sem, device_id=where
        ).wait_recv()

    send(mixed, rim, rim_send, rim_recv, {"ctx": after})
    for bits in range(1, TP):
        send(
            gain_ref, gains.at[bits], gain_send.at[bits], gain_recv.at[bits],
            {"tp": flipped(tp, bits)},
        )
    gains[0] = gain_ref[...]

    own = mixed[...].astype(F32)
    for r in range(8):
        shifted[r, pl.ds(ROWS, ROWS), :] = own if r == 0 else pltpu.roll(own, r, 0)

    def tap_sum(q, start, count):
        out = None
        for r in range(8):
            part = taps_ref[pl.ds(8 * q + r, 1), :] * shifted[r, pl.ds(start, count), :]
            out = part if out is None else out + part
        return out

    filtered[...] = jnp.zeros((ROWS, CH), F32)
    for q in range(15):
        first = 8 * (q + 1)
        filtered[pl.ds(first, ROWS - first), :] += tap_sum(q, ROWS + 8, ROWS - first)

    arrived(rim, rim_send, rim_recv, {"ctx": before})
    kept = (c > 0).astype(F32)
    joined = jnp.concatenate([rim[...].astype(F32) * kept, own[:8]], axis=0)
    for r in range(8):
        shifted[r, pl.ds(0, ROWS + 8), :] = joined if r == 0 else pltpu.roll(joined, r, 0)
    for q in range(16):
        filtered[pl.ds(0, 8 * (q + 1)), :] += tap_sum(q, ROWS - 8 * q, 8 * (q + 1))

    xall[0] = (gate_ref[...].astype(F32) * filtered[...]).astype(BF16)

    def push(slot, bits):
        send(
            xall.at[slot], xall.at[slot ^ bits], x_send.at[len(sent)], x_recv.at[slot ^ bits],
            {"tp": flipped(tp, bits)},
        )

    def push_half(slot, half, bits):
        rows = pl.ds(64 * half, 64)
        send(
            xall.at[slot, rows], xall.at[slot ^ bits, rows],
            half_send.at[slot // 8, half], half_recv.at[slot // 8, half],
            {"tp": flipped(tp, bits)},
        )

    def await_slot(slot):
        if slot % 8 == 4:
            for half in range(2):
                rows = xall.at[slot, pl.ds(64 * half, 64)]
                arrived(
                    rows, half_send.at[slot // 8, half], half_recv.at[slot // 8, half],
                    {"tp": flipped(tp, 2)},
                )
        else:
            arrived(xall.at[slot], x_send.at[0], x_recv.at[slot], {"tp": flipped(tp, 1)})

    def absorb(slot):
        h = xall[slot].astype(F32)
        squared = h * h
        part = squared[:, :128] + squared[:, 128:]
        squares[...] = part if slot == 0 else squares[...] + part
        x = (h * gains[slot]).astype(BF16)
        start = pl.multiple_of(flipped(tp, slot) * CH, CH)
        for i in range(3):
            added = jnp.dot(x, w_ref[i, pl.ds(start, CH), :], preferred_element_type=F32)
            proj[i] = added if slot == 0 else proj[i] + added

    for bits in (8, 2, 6, 1):
        push(0, bits)
    w_copy.wait()
    absorb(0)
    for bits in range(1, TP):
        arrived(gains.at[bits], gain_send.at[bits], gain_recv.at[bits], {"tp": flipped(tp, bits)})
    await_slot(1)
    absorb(1)
    await_slot(2)
    push_half(2, 0, 6)
    push(2, 1)
    await_slot(6)
    push_half(6, 1, 2)
    push(6, 1)
    absorb(2)
    absorb(6)
    await_slot(8)
    push(8, 2)
    push(8, 6)
    push(8, 1)
    await_slot(4)
    push(4, 1)
    absorb(8)
    absorb(4)
    await_slot(3)
    absorb(3)
    await_slot(7)
    absorb(7)
    await_slot(10)
    push_half(10, 0, 6)
    push(10, 1)
    await_slot(14)
    push_half(14, 1, 2)
    push(14, 1)
    absorb(10)
    absorb(14)
    await_slot(9)
    absorb(9)
    await_slot(5)
    absorb(5)
    await_slot(12)
    push(12, 1)
    absorb(12)
    for slot in (11, 15, 13):
        await_slot(slot)
        absorb(slot)

    msq = jnp.sum(squares[...], axis=1, keepdims=True) / D
    factor = lax.rsqrt(msq + 1e-06)
    kv[c] = jnp.concatenate([proj[1] * factor, proj[2] * factor], axis=1).astype(BF16)
    q_ref[...] = (proj[0] * factor).astype(BF16)

    counter = [0]
    piece_rows = ROWS // PIECES

    def pass_on(source, direction, lane, step, piece, other):
        block = kv.at[source, pl.ds(piece * piece_rows, piece_rows)]
        send(
            block, block, kv_send.at[counter[0]],
            kv_recv.at[direction, lane, step, piece], {"ctx": other},
        )
        counter[0] += 1

    def await_block(source, direction, lane, step, piece):
        block = kv.at[source, pl.ds(piece * piece_rows, piece_rows)]
        arrived(block, kv_send.at[0], kv_recv.at[direction, lane, step, piece], {"ctx": partner})

    def source_of(first_index, direction, step):
        move = CTX - 2 * step if direction == 0 else 2 * step
        return (first_index + move) % CTX

    row_pos = c * ROWS + lax.broadcasted_iota(jnp.int32, (ROWS, 256), 0)
    key_iota = lax.broadcasted_iota(jnp.int32, (ROWS, 256), 1)
    scale = 1.0 / math.sqrt(HEAD_DIM)

    def attend(z_source, initial=False):
        pair = kv[pl.ds(2 * z_source, 2)].reshape(256, 256)
        scores = (
            lax.dot_general(
                q_ref[...], pair[:, :128], (((1,), (1,)), ((), ())), preferred_element_type=F32
            )
            * scale
        )
        allowed = row_pos >= key_iota + z_source * 256
        scores = jnp.where(allowed, scores, -1e30)
        block_top = jnp.max(scores, axis=1, keepdims=True)
        new_top = block_top if initial else jnp.maximum(top[...], block_top)
        expo = jnp.where(allowed, jnp.exp(scores - new_top), 0.0)
        block_total = jnp.sum(expo, axis=1, keepdims=True)
        added = jnp.dot(expo.astype(BF16), pair[:, 128:], preferred_element_type=F32)
        if initial:
            total[...] = block_total
            acc[...] = added
        else:
            fade = jnp.exp(top[...] - new_top)
            total[...] = total[...] * fade + block_total
            acc[...] = acc[...] * fade + added
        top[...] = new_top

    def attend_step(step):
        @pl.when(z >= step)
        def _():
            attend((z + NZ - step) % NZ)

        if step < 8:
            @pl.when(z + step >= NZ)
            def _():
                attend((z + step) % NZ)

    def spread(source, direction, lane, step, piece, limit):
        for far in sorted(PARENT, reverse=True):
            if PARENT[far] == step and far <= limit:
                pass_on(source, direction, lane, far, piece, along(direction, far - step))

    def last(direction, piece):
        return 8 if (piece < (PIECES + 1) // 2) == (direction == 0) else 7

    for piece in range(PIECES):
        for direction in range(2):
            spread(c, direction, 0, 0, piece, last(direction, piece))
        pass_on(c, 0, 1, 0, piece, partner)
    for piece in range(PIECES):
        await_block(partner, 0, 1, 0, piece)
        for direction in range(2):
            spread(partner, direction, 1, 0, piece, NEAR)
    attend(z, initial=True)
    for step in range(1, 10):
        for piece in range(PIECES):
            for direction in range(2):
                if step <= last(direction, piece):
                    source = source_of(c, direction, step)
                    await_block(source, direction, 0, step, piece)
                    spread(source, direction, 0, step, piece, last(direction, piece))
                    if step > NEAR:
                        pass_on(source, direction, 1, step, piece, partner)
        ready = step if step <= NEAR else step - 1
        if step == NEAR + 1:
            continue
        for piece in range(PIECES):
            for direction in range(2):
                if ready <= last(direction, piece):
                    source = source_of(partner, direction, ready)
                    await_block(source, direction, 1, ready, piece)
                    spread(source, direction, 1, ready, piece, NEAR)
        attend_step(ready)

    out_ref[...] = (acc[...] / total[...]).astype(BF16)
    for copy in sent:
        copy.wait_send()


def body(gate_in, conv_in, value_in, filter_taps, norm_gain, qkv_weight):
    vmem = pl.BlockSpec(memory_space=pltpu.VMEM)
    dma = pltpu.SemaphoreType.DMA
    return pl.pallas_call(
        kernel,
        out_shape=jax.ShapeDtypeStruct((ROWS, HEAD_DIM), BF16),
        in_specs=[vmem] * 5 + [pl.BlockSpec(memory_space=pl.ANY)],
        out_specs=vmem,
        scratch_shapes=[
            pltpu.VMEM((ROWS, CH), BF16),
            pltpu.VMEM((ROWS, CH), BF16),
            pltpu.VMEM((8, 2 * ROWS, CH), F32),
            pltpu.VMEM((ROWS, CH), F32),
            pltpu.VMEM((TP, ROWS, CH), BF16),
            pltpu.VMEM((TP, 1, CH), F32),
            pltpu.VMEM((3, D, HEAD_DIM), BF16),
            pltpu.VMEM((CTX, ROWS, 2 * HEAD_DIM), BF16),
            pltpu.VMEM((ROWS, HEAD_DIM), BF16),
            pltpu.VMEM((3, ROWS, HEAD_DIM), F32),
            pltpu.VMEM((ROWS, HEAD_DIM), F32),
            pltpu.VMEM((ROWS, 1), F32),
            pltpu.VMEM((ROWS, 1), F32),
            pltpu.VMEM((ROWS, HEAD_DIM), F32),
            dma,
            dma,
            dma,
            dma((TP,)),
            dma((TP,)),
            dma((48,)),
            dma((TP,)),
            dma((2, 2)),
            dma((2, 2)),
            dma((32 * PIECES,)),
            dma((2, 2, 9, PIECES)),
        ],
        compiler_params=pltpu.CompilerParams(collective_id=0, has_side_effects=True),
    )(
        gate_in, conv_in, value_in, filter_taps, norm_gain.reshape(1, CH),
        jnp.transpose(qkv_weight, (1, 0, 2)),
    )


def solution(mesh):
    placed = (
        P("ctx", "tp"),
        P("ctx", "tp"),
        P("ctx", "tp"),
        P(None, "tp"),
        P("tp"),
        P(None, None, "tp"),
    )
    return jax.shard_map(
        body, mesh=mesh, in_specs=placed, out_specs=P("ctx", "tp"), check_vma=False
    )
```

```python
import math

import jax
import jax.numpy as jnp
from jax import lax
from jax.experimental import pallas as pl
from jax.experimental.pallas import tpu as pltpu
from jax.sharding import PartitionSpec as P

D = 4096
HEAD_DIM = 128
ROWS = 128
CH = 256
CTX = 32
TP = 16
NZ = 16
NEAR = 1
PIECES = 2
PARENT = {far: far - 1 for far in range(1, 9)}
HOPS = sorted({far - near for far, near in PARENT.items()})
F32 = jnp.float32
BF16 = jnp.bfloat16


def flipped(index, bits):
    out = index
    for bit in (1, 2, 4, 8):
        if bits & bit:
            out = out + bit - 2 * bit * ((index // bit) % 2)
    return out


def kernel(
    gate_ref, conv_ref, value_ref, taps_ref, gain_ref, w_hbm, out_ref,
    mixed, rim, shifted, filtered, xall, gains, w_ref, kv, q_ref, proj, squares,
    top, total, acc,
    w_sem, rim_send, rim_recv, gain_send, gain_recv,
    x_send, x_recv, half_send, half_recv, kv_send, kv_recv,
):
    c = lax.axis_index("ctx")
    tp = lax.axis_index("tp")
    z = c // 2
    partner = c + 1 - 2 * (c % 2)
    after = (c + 1) % CTX
    before = (c + CTX - 1) % CTX

    def along(direction, hops):
        return (c + (2 * hops if direction == 0 else CTX - 2 * hops)) % CTX


    w_copy = pltpu.make_async_copy(w_hbm, w_ref, w_sem)
    w_copy.start()

    barrier = pltpu.get_barrier_semaphore()
    for bits in range(1, TP):
        pl.semaphore_signal(barrier, inc=1, device_id={"tp": flipped(tp, bits)})
    ringed = [along(direction, hops) for hops in HOPS for direction in range(2)]
    for other in [after, before, partner] + ringed:
        pl.semaphore_signal(barrier, inc=1, device_id={"ctx": other})
    mixed[...] = (conv_ref[...].astype(F32) * value_ref[...].astype(F32)).astype(BF16)
    pl.semaphore_wait(barrier, TP - 1 + 3 + 2 * len(HOPS))

    sent = []

    def send(src, dst, send_sem, recv_sem, where):
        copy = pltpu.make_async_remote_copy(
            src_ref=src, dst_ref=dst, send_sem=send_sem, recv_sem=recv_sem, device_id=where
        )
        copy.start()
        sent.append(copy)

    def arrived(dst, send_sem, recv_sem, where):
        pltpu.make_async_remote_copy(
            src_ref=dst, dst_ref=dst, send_sem=send_sem, recv_sem=recv_sem, device_id=where
        ).wait_recv()

    send(mixed, rim, rim_send, rim_recv, {"ctx": after})
    for bits in range(1, TP):
        send(
            gain_ref, gains.at[bits], gain_send.at[bits], gain_recv.at[bits],
            {"tp": flipped(tp, bits)},
        )
    gains[0] = gain_ref[...]

    own = mixed[...].astype(F32)
    for r in range(8):
        shifted[r, pl.ds(ROWS, ROWS), :] = own if r == 0 else pltpu.roll(own, r, 0)

    def tap_sum(q, start, count):
        out = None
        for r in range(8):
            part = taps_ref[pl.ds(8 * q + r, 1), :] * shifted[r, pl.ds(start, count), :]
            out = part if out is None else out + part
        return out

    filtered[...] = jnp.zeros((ROWS, CH), F32)
    for q in range(15):
        first = 8 * (q + 1)
        filtered[pl.ds(first, ROWS - first), :] += tap_sum(q, ROWS + 8, ROWS - first)

    arrived(rim, rim_send, rim_recv, {"ctx": before})
    kept = (c > 0).astype(F32)
    joined = jnp.concatenate([rim[...].astype(F32) * kept, own[:8]], axis=0)
    for r in range(8):
        shifted[r, pl.ds(0, ROWS + 8), :] = joined if r == 0 else pltpu.roll(joined, r, 0)
    for q in range(16):
        filtered[pl.ds(0, 8 * (q + 1)), :] += tap_sum(q, ROWS - 8 * q, 8 * (q + 1))

    xall[0] = (gate_ref[...].astype(F32) * filtered[...]).astype(BF16)

    def push(slot, bits):
        send(
            xall.at[slot], xall.at[slot ^ bits], x_send.at[len(sent)], x_recv.at[slot ^ bits],
            {"tp": flipped(tp, bits)},
        )

    def push_half(slot, half, bits):
        rows = pl.ds(64 * half, 64)
        send(
            xall.at[slot, rows], xall.at[slot ^ bits, rows],
            half_send.at[slot // 8, half], half_recv.at[slot // 8, half],
            {"tp": flipped(tp, bits)},
        )

    def await_slot(slot):
        if slot == 4:
            for half in range(2):
                rows = xall.at[slot, pl.ds(64 * half, 64)]
                arrived(
                    rows, half_send.at[slot // 8, half], half_recv.at[slot // 8, half],
                    {"tp": flipped(tp, 2)},
                )
        else:
            arrived(xall.at[slot], x_send.at[0], x_recv.at[slot], {"tp": flipped(tp, 1)})

    def absorb(slot):
        h = xall[slot].astype(F32)
        squared = h * h
        part = squared[:, :128] + squared[:, 128:]
        squares[...] = part if slot == 0 else squares[...] + part
        x = (h * gains[slot]).astype(BF16)
        start = pl.multiple_of(flipped(tp, slot) * CH, CH)
        for i in range(3):
            added = jnp.dot(x, w_ref[i, pl.ds(start, CH), :], preferred_element_type=F32)
            proj[i] = added if slot == 0 else proj[i] + added

    for bits in (8, 2, 6, 1):
        push(0, bits)
    w_copy.wait()
    absorb(0)
    for bits in range(1, TP):
        arrived(gains.at[bits], gain_send.at[bits], gain_recv.at[bits], {"tp": flipped(tp, bits)})
    await_slot(1)
    absorb(1)
    await_slot(2)
    push_half(2, 0, 6)
    push(2, 1)
    await_slot(6)
    push_half(6, 1, 2)
    push(6, 1)
    absorb(2)
    absorb(6)
    await_slot(8)
    push(8, 2)
    push(8, 6)
    push(8, 4)
    push(8, 1)
    await_slot(4)
    push(4, 1)
    absorb(8)
    absorb(4)
    await_slot(3)
    absorb(3)
    await_slot(7)
    absorb(7)
    await_slot(10)
    push(10, 1)
    await_slot(14)
    push(14, 1)
    absorb(10)
    absorb(14)
    await_slot(9)
    absorb(9)
    await_slot(5)
    absorb(5)
    await_slot(12)
    push(12, 1)
    absorb(12)
    for slot in (11, 15, 13):
        await_slot(slot)
        absorb(slot)

    msq = jnp.sum(squares[...], axis=1, keepdims=True) / D
    factor = lax.rsqrt(msq + 1e-06)
    kv[c] = jnp.concatenate([proj[1] * factor, proj[2] * factor], axis=1).astype(BF16)
    q_ref[...] = (proj[0] * factor).astype(BF16)

    counter = [0]
    piece_rows = ROWS // PIECES

    def pass_on(source, direction, lane, step, piece, other):
        block = kv.at[source, pl.ds(piece * piece_rows, piece_rows)]
        send(
            block, block, kv_send.at[counter[0]],
            kv_recv.at[direction, lane, step, piece], {"ctx": other},
        )
        counter[0] += 1

    def await_block(source, direction, lane, step, piece):
        block = kv.at[source, pl.ds(piece * piece_rows, piece_rows)]
        arrived(block, kv_send.at[0], kv_recv.at[direction, lane, step, piece], {"ctx": partner})

    def source_of(first_index, direction, step):
        move = CTX - 2 * step if direction == 0 else 2 * step
        return (first_index + move) % CTX

    row_pos = c * ROWS + lax.broadcasted_iota(jnp.int32, (ROWS, 256), 0)
    key_iota = lax.broadcasted_iota(jnp.int32, (ROWS, 256), 1)
    scale = 1.0 / math.sqrt(HEAD_DIM)

    def attend(z_source, initial=False):
        pair = kv[pl.ds(2 * z_source, 2)].reshape(256, 256)
        scores = (
            lax.dot_general(
                q_ref[...], pair[:, :128], (((1,), (1,)), ((), ())), preferred_element_type=F32
            )
            * scale
        )
        allowed = row_pos >= key_iota + z_source * 256
        scores = jnp.where(allowed, scores, -1e30)
        block_top = jnp.max(scores, axis=1, keepdims=True)
        new_top = block_top if initial else jnp.maximum(top[...], block_top)
        expo = jnp.where(allowed, jnp.exp(scores - new_top), 0.0)
        block_total = jnp.sum(expo, axis=1, keepdims=True)
        added = jnp.dot(expo.astype(BF16), pair[:, 128:], preferred_element_type=F32)
        if initial:
            total[...] = block_total
            acc[...] = added
        else:
            fade = jnp.exp(top[...] - new_top)
            total[...] = total[...] * fade + block_total
            acc[...] = acc[...] * fade + added
        top[...] = new_top

    def attend_step(step):
        @pl.when(z >= step)
        def _():
            attend((z + NZ - step) % NZ)

        if step < 8:
            @pl.when(z + step >= NZ)
            def _():
                attend((z + step) % NZ)

    def spread(source, direction, lane, step, piece, limit):
        for far in sorted(PARENT, reverse=True):
            if PARENT[far] == step and far <= limit:
                pass_on(source, direction, lane, far, piece, along(direction, far - step))

    def last(direction, piece):
        return 8 if (piece < (PIECES + 1) // 2) == (direction == 0) else 7

    for piece in range(PIECES):
        for direction in range(2):
            spread(c, direction, 0, 0, piece, last(direction, piece))
        pass_on(c, 0, 1, 0, piece, partner)
    for piece in range(PIECES):
        await_block(partner, 0, 1, 0, piece)
        for direction in range(2):
            spread(partner, direction, 1, 0, piece, NEAR)
    attend(z, initial=True)
    for step in range(1, 10):
        for piece in range(PIECES):
            for direction in range(2):
                if step <= last(direction, piece):
                    source = source_of(c, direction, step)
                    await_block(source, direction, 0, step, piece)
                    spread(source, direction, 0, step, piece, last(direction, piece))
                    if step > NEAR:
                        pass_on(source, direction, 1, step, piece, partner)
        ready = step if step <= NEAR else step - 1
        if step == NEAR + 1:
            continue
        for piece in range(PIECES):
            for direction in range(2):
                if ready <= last(direction, piece):
                    source = source_of(partner, direction, ready)
                    await_block(source, direction, 1, ready, piece)
                    spread(source, direction, 1, ready, piece, NEAR)
        attend_step(ready)

    out_ref[...] = (acc[...] / total[...]).astype(BF16)
    for copy in sent:
        copy.wait_send()


def body(gate_in, conv_in, value_in, filter_taps, norm_gain, qkv_weight):
    vmem = pl.BlockSpec(memory_space=pltpu.VMEM)
    dma = pltpu.SemaphoreType.DMA
    return pl.pallas_call(
        kernel,
        out_shape=jax.ShapeDtypeStruct((ROWS, HEAD_DIM), BF16),
        in_specs=[vmem] * 5 + [pl.BlockSpec(memory_space=pl.ANY)],
        out_specs=vmem,
        scratch_shapes=[
            pltpu.VMEM((ROWS, CH), BF16),
            pltpu.VMEM((ROWS, CH), BF16),
            pltpu.VMEM((8, 2 * ROWS, CH), F32),
            pltpu.VMEM((ROWS, CH), F32),
            pltpu.VMEM((TP, ROWS, CH), BF16),
            pltpu.VMEM((TP, 1, CH), F32),
            pltpu.VMEM((3, D, HEAD_DIM), BF16),
            pltpu.VMEM((CTX, ROWS, 2 * HEAD_DIM), BF16),
            pltpu.VMEM((ROWS, HEAD_DIM), BF16),
            pltpu.VMEM((3, ROWS, HEAD_DIM), F32),
            pltpu.VMEM((ROWS, HEAD_DIM), F32),
            pltpu.VMEM((ROWS, 1), F32),
            pltpu.VMEM((ROWS, 1), F32),
            pltpu.VMEM((ROWS, HEAD_DIM), F32),
            dma,
            dma,
            dma,
            dma((TP,)),
            dma((TP,)),
            dma((48,)),
            dma((TP,)),
            dma((2, 2)),
            dma((2, 2)),
            dma((32 * PIECES,)),
            dma((2, 2, 9, PIECES)),
        ],
        compiler_params=pltpu.CompilerParams(collective_id=0, has_side_effects=True),
    )(
        gate_in, conv_in, value_in, filter_taps, norm_gain.reshape(1, CH),
        jnp.transpose(qkv_weight, (1, 0, 2)),
    )


def solution(mesh):
    placed = (
        P("ctx", "tp"),
        P("ctx", "tp"),
        P("ctx", "tp"),
        P(None, "tp"),
        P("tp"),
        P(None, None, "tp"),
    )
    return jax.shard_map(
        body, mesh=mesh, in_specs=placed, out_specs=P("ctx", "tp"), check_vma=False
    )
```
